256 devices in a mesh: seq: 64 (over y, z_hi, x), ch: 4 (over z_lo, core).
Axes of the slice: x: 4, y: 4, z: 8 (z_hi: 4, z_lo: 2; z = z_hi * 2 + z_lo), core: 2. Of those that a mesh axis runs over, the one named last changes fastest.
Arguments:
- features: bfloat16 [16384, 3, 2048], P('seq', None, 'ch'), may hold values from -6 to 6
- short_weight: float32 [3, 3, 2048], P(None, None, 'ch'), may hold values from -3 to 3
- residue: float32 [2048, 16], P('ch'), may hold values from -1.5 to 1.5
- decay_rate: float32 [2048, 16], P('ch'), may hold values from 1.5258789e-05 to 0.04
- skip_gain: float32 [2048], P('ch'), may hold values from -2.5 to 2.5
- out_weight: bfloat16 [2048, 4096], P('ch'), may hold values from -0.125 to 0.125
- out_grad: bfloat16 [16384, 4096], P('seq', 'ch'), may hold values from -6 to 6
Outputs:
- block_out: bfloat16 [16384, 4096], P('seq', 'ch')
- feature_grad: bfloat16 [16384, 3, 2048], P('seq', None, 'ch')
- short_grad: float32 [3, 3, 2048], P(None, None, 'ch')
- residue_grad: float32 [2048, 16], P('ch')
- skip_grad: float32 [2048], P('ch')
- weight_grad: bfloat16 [4096, 2048], P('seq', 'ch')
The draws below stay inside these ranges and needn't reach their ends.
All inputs are finite; a program needn't handle non-finite values.
Results may differ from the reference program's by a relative error of at most 0.012.
Values may be sent and summed in bfloat16 or wider, within the bound.
No kernel may reach another device: no remote copies, remote signals or barrier semaphores. Data moves between devices by JAX's collectives and lax.ppermute only.
A program may use at most 128 MiB of HBM per device.

```python
import math
import jax
import jax.numpy as jnp
from jax import lax

D = 4096
HC = 2048
RK = 16
KS = 3
TOKENS = 16384


def block_scale(stream_key, shape, split, smallest, top_value):
    loudness = 1.0
    for position, blocks in split:
        steps = jax.random.uniform(jax.random.fold_in(jax.random.fold_in(stream_key, 6), position), (blocks,), jnp.float32, smallest / len(split), top_value / len(split))
        loudness = loudness * jnp.repeat(jnp.exp(steps), shape[position] // blocks).reshape((-1,) + (1,) * (len(shape) - 1 - position))
    return loudness


def scatter_about(rng, shape, width, most, shards=(), held_as=jnp.bfloat16):
    values = jax.random.normal(rng, shape, jnp.float32) * width
    if len(shards) > 0:
        values = block_scale(rng, shape, shards, -0.22, 0.18) * values
    return jnp.clip(values, min=-most, max=most).astype(held_as)


def setup_inputs(seed: int = 0) -> dict:
    splits = jax.random.split(jax.random.key(seed), 8)
    features = scatter_about(splits[0], (TOKENS, 3, HC), 1.0, 6.0, ((0, 64), (2, 4)))
    short_weight = scatter_about(splits[1], (3, KS, HC), 0.6, 3.0, ((2, 4),), jnp.float32)
    residue = scatter_about(splits[2], (HC, RK), 0.25, 1.5, ((0, 4),), jnp.float32)
    decay_rate = jnp.clip(jnp.exp(math.log(0.04) - 7.871479 * jax.random.uniform(splits[3], (HC, RK), jnp.float32) ** block_scale(splits[3], (HC, RK), ((0, 4),), -0.2, 0.2)), 1.52587890625e-05, 0.04)
    skip_gain = scatter_about(splits[4], (HC,), 0.5, 2.5, ((0, 4),), jnp.float32)
    out_weight = scatter_about(splits[5], (HC, D), HC ** -0.5, 0.125, ((0, 4),))
    out_grad = scatter_about(splits[6], (TOKENS, D), 1.0, 6.0, ((0, 64), (1, 4)))
    return dict(features=features, short_weight=short_weight, residue=residue, decay_rate=decay_rate, skip_gain=skip_gain, out_weight=out_weight, out_grad=out_grad)


def causal_block(signal, residue, decay_rate):
    length = signal.shape[1]
    times = jnp.arange(length).astype(jnp.float32)
    powers = jnp.exp(-decay_rate[:, :, None] * times)
    amplitude = residue * jnp.sqrt(2.0 * decay_rate)
    kernel = jnp.einsum('cr,crt->ct', amplitude, powers)
    spectrum = jnp.fft.rfft(kernel, n=2 * length) * jnp.fft.rfft(signal, n=2 * length)
    return jnp.fft.irfft(spectrum, n=2 * length)[:, :length]

def anticausal_block(signal, residue, decay_rate):
    return causal_block(signal[:, ::-1], residue, decay_rate)[:, ::-1]

def correlation_block(gradient, signal, residue, decay_rate):
    length = signal.shape[1]
    spectrum = jnp.fft.rfft(gradient, n=2 * length) * jnp.conj(jnp.fft.rfft(signal, n=2 * length))
    lagged = jnp.fft.irfft(spectrum, n=2 * length)[:, :length]
    times = jnp.arange(length).astype(jnp.float32)
    powers = jnp.exp(-decay_rate[:, :, None] * times)
    return jnp.sqrt(2.0 * decay_rate) * jnp.einsum('ct,crt->cr', lagged, powers)

def by_channels(work, fields, params):
    channels = fields[0].shape[1]
    length = fields[0].shape[0]
    group = min(32, channels)
    stacked = [field.T.reshape(channels // group, group, length) for field in fields]
    grouped = [param.reshape(channels // group, group, param.shape[1]) for param in params]
    return lax.map(lambda items: work(*items), tuple(stacked + grouped))

def reference(features, short_weight, residue, decay_rate, skip_gain, out_weight, out_grad):
    tokens = features.shape[0]
    channels = features.shape[2]
    kernel_taps = short_weight.shape[1]
    grad_scale = 1.0 / math.sqrt(TOKENS)
    feature_float = features.astype(jnp.float32)
    padded = jnp.concatenate([jnp.zeros((kernel_taps - 1, 3, channels), jnp.float32), feature_float], axis=0)
    filtered = jnp.zeros_like(feature_float)
    for shift_index in range(kernel_taps):
        start_row = kernel_taps - 1 - shift_index
        filtered = filtered + short_weight[:, shift_index, :] * padded[start_row:start_row + tokens]
    queries = filtered[:, 0]
    key_field = filtered[:, 1]
    value_field = filtered[:, 2]
    product = (key_field * value_field).astype(jnp.bfloat16)
    product_float = product.astype(jnp.float32)
    conv_part = by_channels(causal_block, [product_float], [residue, decay_rate]).reshape(channels, tokens).T
    gated_mix = (conv_part + skip_gain * product_float).astype(jnp.bfloat16)
    gated_float = gated_mix.astype(jnp.float32)
    mixed_out = (queries * gated_float).astype(jnp.bfloat16)
    block_out = jnp.dot(mixed_out, out_weight, preferred_element_type=jnp.float32).astype(jnp.bfloat16)
    mixed_grad = lax.dot_general(out_grad, out_weight, (((1,), (1,)), ((), ())), preferred_element_type=jnp.float32)
    gate_grad = (mixed_grad * queries).astype(jnp.bfloat16)
    gate_float = gate_grad.astype(jnp.float32)
    query_grad = mixed_grad * gated_float
    back_part = by_channels(anticausal_block, [gate_float], [residue, decay_rate]).reshape(channels, tokens).T
    product_grad = (back_part + skip_gain * gate_float).astype(jnp.bfloat16)
    product_back = product_grad.astype(jnp.float32)
    filtered_grad = jnp.stack([query_grad, product_back * value_field, product_back * key_field], axis=1)
    padded_grad = jnp.concatenate([filtered_grad, jnp.zeros((kernel_taps - 1, 3, channels), jnp.float32)], axis=0)
    feature_grad = jnp.zeros_like(filtered_grad)
    short_terms = []
    for shift_index in range(kernel_taps):
        start_row = kernel_taps - 1 - shift_index
        feature_grad = feature_grad + short_weight[:, shift_index, :] * padded_grad[shift_index:shift_index + tokens]
        short_terms.append(lax.optimization_barrier(jnp.sum(filtered_grad * padded[start_row:start_row + tokens], axis=0)))
    short_grad = jnp.stack(short_terms, axis=1) * grad_scale
    residue_grad = by_channels(correlation_block, [gate_float, product_float], [residue, decay_rate]).reshape(channels, residue.shape[1]) * grad_scale
    skip_grad = lax.optimization_barrier(jnp.sum(gate_float * product_float, axis=0)) * grad_scale
    weight_grad = (lax.dot_general(out_grad, mixed_out, (((0,), (0,)), ((), ())), preferred_element_type=jnp.float32) * grad_scale).astype(jnp.bfloat16)
    return (block_out, feature_grad.astype(jnp.bfloat16), short_grad, residue_grad, skip_grad, weight_grad)
```

```python
import functools
import math

import jax
import jax.numpy as jnp
from jax import lax
from jax.experimental import pallas as pl
from jax.experimental.pallas import tpu as pltpu
from jax.sharding import Mesh, PartitionSpec as P

F32 = jnp.float32
BF16 = jnp.bfloat16
SEQ = ("y", "zh", "x")
CH = ("zl", "core")
LEVELS = ("x", "zh", "y")
CHUNKS = 8
LANES = 128
INTERPRET = False


def cyclic(value, axis, distance):
    size = lax.axis_size(axis)
    return lax.ppermute(value, axis, [(i, (i + distance) % size) for i in range(size)])


def from_behind(block, distance):
    count = lax.axis_size(SEQ)
    route = [(i - distance, i) for i in range(count) if 0 <= i - distance < count]
    return lax.ppermute(block, SEQ, route)


def run_states(x_ref, decays, states, steps, reverse):
    def step(i, carried):
        t = steps - 1 - i if reverse else i
        row = x_ref[pl.ds(t, CHUNKS, stride=steps), :]
        return tuple(d * h + row for d, h in zip(decays, carried))

    return lax.fori_loop(0, steps, step, states, unroll=4)


def ends_kernel(reverse, x_ref, rate_ref, end_ref, chunk_ref):
    modes = rate_ref.shape[0]
    steps = x_ref.shape[0] // CHUNKS
    shape = (CHUNKS, x_ref.shape[1])
    chunk = lax.broadcasted_iota(jnp.int32, shape, 0).astype(F32)
    away = chunk if reverse else (CHUNKS - 1.0) - chunk
    rates = [jnp.broadcast_to(rate_ref[r : r + 1, :], shape) for r in range(modes)]
    decays = [jnp.exp(-rate) for rate in rates]
    zero = tuple(jnp.zeros(shape, F32) for _ in range(modes))
    states = run_states(x_ref, decays, zero, steps, reverse)
    for r in range(modes):
        chunk_ref[r] = states[r]
        weight = jnp.exp(-rates[r] * (away * float(steps)))
        end_ref[r : r + 1, :] = jnp.sum(states[r] * weight, axis=0, keepdims=True)


def entering_states(chunk_ref, enter_ref, rates, steps, reverse):
    shape = chunk_ref.shape[1:]
    index = lax.broadcasted_iota(jnp.int32, shape, 0)
    from_edge = (CHUNKS - 1) - index if reverse else index
    away = from_edge.astype(F32)
    result = []
    for r, rate in enumerate(rates):
        total = chunk_ref[r]
        for hop in (1, 2, 4):
            moved = pltpu.roll(total, CHUNKS - hop if reverse else hop, 0)
            scaled = moved * jnp.exp(-rate * float(steps * hop))
            total = total + jnp.where(from_edge >= hop, scaled, 0.0)
        moved = pltpu.roll(total, CHUNKS - 1 if reverse else 1, 0)
        inner = jnp.where(from_edge >= 1, moved, 0.0)
        outer = enter_ref[r : r + 1, :] * jnp.exp(-rate * (away * float(steps)))
        result.append(inner + outer)
    return tuple(result)


def forward_kernel(x_ref, rate_ref, amp_ref, skip_ref, chunk_ref, enter_ref, out_ref):
    modes = rate_ref.shape[0]
    steps = x_ref.shape[0] // CHUNKS
    shape = (CHUNKS, x_ref.shape[1])
    rates = [jnp.broadcast_to(rate_ref[r : r + 1, :], shape) for r in range(modes)]
    amps = [jnp.broadcast_to(amp_ref[r : r + 1, :], shape) for r in range(modes)]
    skip = jnp.broadcast_to(skip_ref[...], shape)
    states = entering_states(chunk_ref, enter_ref, rates, steps, False)
    decays = [jnp.exp(-rate) for rate in rates]

    def step(t, carried):
        row = x_ref[pl.ds(t, CHUNKS, stride=steps), :]
        total = skip * row
        after = []
        for r in range(modes):
            state = decays[r] * carried[r] + row
            total = total + amps[r] * state
            after.append(state)
        out_ref[pl.ds(t, CHUNKS, stride=steps), :] = total
        return tuple(after)

    lax.fori_loop(0, steps, step, states, unroll=2)


def backward_kernel(
    g_ref, x_ref, rate_ref, amp_ref, skip_ref, chunk_ref, enter_ref, out_ref, res_ref, sum_ref
):
    modes = rate_ref.shape[0]
    steps = g_ref.shape[0] // CHUNKS
    shape = (CHUNKS, g_ref.shape[1])
    rates = [jnp.broadcast_to(rate_ref[r : r + 1, :], shape) for r in range(modes)]
    amps = [jnp.broadcast_to(amp_ref[r : r + 1, :], shape) for r in range(modes)]
    skip = jnp.broadcast_to(skip_ref[...], shape)
    states = entering_states(chunk_ref, enter_ref, rates, steps, True)
    decays = [jnp.exp(-rate) for rate in rates]
    zero = jnp.zeros(shape, F32)

    def step(i, carried):
        held, sums, direct = carried
        t = steps - 1 - i
        row = g_ref[pl.ds(t, CHUNKS, stride=steps), :]
        other = x_ref[pl.ds(t, CHUNKS, stride=steps), :]
        total = skip * row
        after = []
        grown = []
        for r in range(modes):
            state = decays[r] * held[r] + row
            total = total + amps[r] * state
            after.append(state)
            grown.append(sums[r] + other * state)
        out_ref[pl.ds(t, CHUNKS, stride=steps), :] = total
        return tuple(after), tuple(grown), direct + row * other

    _, sums, direct = lax.fori_loop(0, steps, step, (states, (zero,) * modes, zero))
    for r in range(modes):
        res_ref[r : r + 1, :] = jnp.sum(sums[r], axis=0, keepdims=True)
    sum_ref[...] = jnp.sum(direct, axis=0, keepdims=True)


def tile_spec(*lead):
    shape = lead + (LANES,)
    return pl.BlockSpec(shape, lambda i, n=len(lead): (0,) * n + (i,))


def tiled_call(kernel, name, width, ins, outs, cost):
    return pl.pallas_call(
        kernel,
        name=name,
        grid=(width // LANES,),
        in_specs=[tile_spec(*lead) for lead in ins],
        out_specs=[tile_spec(*lead) for lead in outs],
        out_shape=[jax.ShapeDtypeStruct(lead + (width,), F32) for lead in outs],
        cost_estimate=pl.CostEstimate(flops=cost, bytes_accessed=cost // 4, transcendentals=0),
        interpret=INTERPRET,
    )


def local_ends(x, rate, reverse):
    rows, width = x.shape
    modes = rate.shape[0]
    call = tiled_call(
        functools.partial(ends_kernel, reverse),
        "ends_bwd" if reverse else "ends_fwd",
        width,
        [(rows,), (modes,)],
        [(modes,), (modes, CHUNKS)],
        rows * width * modes * 2,
    )
    return call(x, rate)


def device_scan(state, rate, length, reverse):
    direction = -1 if reverse else 1
    total = state
    partials = []
    for axis in LEVELS:
        size = lax.axis_size(axis)
        here = lax.axis_index(axis)
        place = size - 1 - here if reverse else here
        prefix = jnp.zeros_like(state)
        whole = jnp.exp(-rate * (length * (size - 1 - place)).astype(F32)) * total
        for k in range(1, size):
            got = cyclic(total, axis, direction * k)
            weight = jnp.where(place >= k, jnp.exp(-rate * float(length * (k - 1))), 0.0)
            prefix = prefix + weight * got
            source = lax.rem(place - k + size, size)
            whole = whole + jnp.exp(-rate * (length * (size - 1 - source)).astype(F32)) * got
        partials.append((prefix, jnp.exp(-rate * (length * place).astype(F32))))
        total = whole
        length *= size
    entering = jnp.zeros_like(state)
    for prefix, decay in reversed(partials):
        entering = prefix + decay * entering
    return entering


def scatter_sum(value, axis):
    size = lax.axis_size(axis)
    here = lax.axis_index(axis)
    total = lax.dynamic_index_in_dim(value, here, 0, False).astype(F32)
    for k in range(1, size):
        block = lax.dynamic_index_in_dim(value, lax.rem(here + k, size), 0, False)
        total = total + cyclic(block, axis, k).astype(F32)
    return total


def all_sum(value):
    for axis in LEVELS:
        total = value
        for k in range(1, lax.axis_size(axis)):
            total = total + cyclic(value, axis, k)
        value = total
    return value


def gather_channels(own):
    over = cyclic(own, "zl", 1)
    beside = cyclic(own, "core", 1)
    across = cyclic(over, "core", 1)
    first = lax.axis_index("core") == 0
    low = lax.axis_index("zl") == 0
    near = [jnp.where(first, own, beside), jnp.where(first, beside, own)]
    far = [jnp.where(first, over, across), jnp.where(first, across, over)]
    parts = [jnp.where(low, a, b) for a, b in zip(near + far, far + near)]
    return jnp.concatenate(parts, axis=1)


def body(features, short_weight, residue, decay_rate, skip_gain, out_weight, out_grad):
    rows, _, width = features.shape
    taps = short_weight.shape[1]
    count = lax.axis_size(SEQ)
    scale = 1.0 / math.sqrt(rows * count)
    streams = jnp.transpose(features, (1, 0, 2))
    before = from_behind(streams[:, rows - (taps - 1) :], 1)
    grad_full = gather_channels(out_grad)
    padded = jnp.concatenate([before, streams], axis=1).astype(F32)
    filtered = jnp.zeros((3, rows, width), F32)
    for j in range(taps):
        start = taps - 1 - j
        filtered = filtered + short_weight[:, j][:, None, :] * padded[:, start : start + rows]
    queries, keys, values = filtered[0], filtered[1], filtered[2]
    product = (keys * values).astype(BF16).astype(F32)
    rate = decay_rate.T
    norm = jnp.sqrt(2.0 * rate)
    amp = residue.T * norm
    skip = skip_gain[None, :]
    modes = rate.shape[0]
    end_f, chunk_f = local_ends(product, rate, False)
    enter_f = device_scan(end_f, rate, rows, False)
    mixed_grad = lax.dot_general(
        grad_full, out_weight, (((1,), (1,)), ((), ())), preferred_element_type=F32
    )
    gate_grad = (mixed_grad * queries).astype(BF16).astype(F32)
    end_b, chunk_b = local_ends(gate_grad, rate, True)
    enter_b = device_scan(end_b, rate, rows, True)

    common = [(modes,), (modes,), (1,), (modes, CHUNKS), (modes,)]
    forward = tiled_call(
        forward_kernel, "conv_fwd", width, [(rows,)] + common, [(rows,)], rows * width * modes * 4
    )
    gated = forward(product, rate, amp, skip, chunk_f, enter_f)[0].astype(BF16).astype(F32)
    mixed_out = (queries * gated).astype(BF16)

    model = grad_full.shape[1]
    half = width // 2
    blocks = (lax.axis_size("y"), lax.axis_size("zh"), lax.axis_size("x"), model // count, half)
    pieces = []
    for part, order in enumerate((("x", "y"), ("y", "x"))):
        share = lax.dot_general(
            grad_full,
            mixed_out[:, part * half : (part + 1) * half],
            (((0,), (0,)), ((), ())),
            preferred_element_type=F32,
        ).astype(BF16)
        share = share.reshape(blocks)
        if order[0] == "x":
            share = jnp.transpose(share, (2, 0, 1, 3, 4))
        else:
            share = jnp.transpose(share, (0, 2, 1, 3, 4))
        for axis in order:
            share = scatter_sum(share, axis).astype(BF16)
        pieces.append(scatter_sum(share, "zh"))
    weight_grad = (jnp.concatenate(pieces, axis=1) * scale).astype(BF16)

    partial = jnp.dot(mixed_out, out_weight, preferred_element_type=F32).astype(BF16)
    quarter = model // 4
    partial = partial.reshape(rows, 2, 2, quarter)
    partial = jnp.transpose(partial, (2, 1, 0, 3))
    block_out = scatter_sum(scatter_sum(partial, "core").astype(BF16), "zl").astype(BF16)

    backward = tiled_call(
        backward_kernel,
        "conv_bwd",
        width,
        [(rows,)] + [(rows,)] + common,
        [(rows,), (modes,), (1,)],
        rows * width * modes * 6,
    )
    back, res_sum, skip_sum = backward(gate_grad, product, rate, amp, skip, chunk_b, enter_b)
    back = back.astype(BF16).astype(F32)
    filtered_grad = jnp.stack([mixed_grad * gated, back * values, back * keys], axis=0)
    after = from_behind(filtered_grad[:, : taps - 1], -1)
    padded_grad = jnp.concatenate([filtered_grad, after], axis=1)
    feature_grad = jnp.zeros_like(filtered_grad)
    terms = []
    for j in range(taps):
        start = taps - 1 - j
        feature_grad = (
            feature_grad + short_weight[:, j][:, None, :] * padded_grad[:, j : j + rows]
        )
        terms.append(jnp.sum(filtered_grad * padded[:, start : start + rows], axis=1))
    short_sum = jnp.stack(terms, axis=1)
    small = jnp.concatenate([short_sum.reshape(3 * taps, width), res_sum, skip_sum], axis=0)
    small = all_sum(small) * scale
    short_grad = small[: 3 * taps].reshape(3, taps, width)
    residue_grad = (small[3 * taps : 3 * taps + modes] * norm).T
    skip_grad = small[3 * taps + modes]
    return (
        block_out,
        jnp.transpose(feature_grad.astype(BF16), (1, 0, 2)),
        short_grad,
        residue_grad,
        skip_grad,
        weight_grad,
    )


def solution(mesh):
    fine = Mesh(mesh.devices.reshape(4, 4, 4, 2, 2), SEQ + CH)
    in_specs = (
        P(SEQ, None, CH),
        P(None, None, CH),
        P(CH, None),
        P(CH, None),
        P(CH),
        P(CH, None),
        P(SEQ, CH),
    )
    out_specs = (
        P(SEQ, CH),
        P(SEQ, None, CH),
        P(None, None, CH),
        P(CH, None),
        P(CH),
        P(SEQ, CH),
    )
    return jax.shard_map(body, mesh=fine, in_specs=in_specs, out_specs=out_specs, check_vma=False)
```
